32 devices in a mesh: ctx: 8 (over z, y), tp: 4 (over x, core).
Axes of the slice: x: 2, y: 2, z: 4, core: 2. Of those that a mesh axis runs over, the one named last changes fastest.
Arguments:
- grad_out: bfloat16 [1024, 8192], P('ctx', 'tp'), may hold values from -40 to 40
- query_in: bfloat16 [1024, 8192], P('ctx', 'tp'), may hold values from -6 to 6
- key_in: bfloat16 [1024, 8192], P('ctx', 'tp'), may hold values from -6 to 6
- value_in: bfloat16 [1024, 8192], P('ctx', 'tp'), may hold values from -6 to 6
- residue: float32 [8192, 16], P('tp'), may hold values from -4 to 4
- log_rate: float32 [8192, 16], P('tp'), may hold values from -14 to -3, as said below
Outputs:
- grad_query: bfloat16 [1024, 8192], P('ctx', 'tp')
- grad_key: bfloat16 [1024, 8192], P('ctx', 'tp')
- grad_value: bfloat16 [1024, 8192], P('ctx', 'tp')
- residue_grad: float32 [8192, 16], P('tp')
- rate_grad: float32 [8192, 16], P('tp')
The draws below stay inside these ranges and needn't reach their ends.
Inputs may be any that keep to these rules, and one draw needn't show every extreme that they name: `log_rate`: exp of an entry is the decay per position of one filter mode.
All inputs are finite; a program needn't handle non-finite values.
Results may differ from the reference program's by a relative error of at most 0.001.
Values sent between devices are 32-bit elements; how exact they have to be, the bound alone decides.
A program may use at most 64 MiB of HBM per device.

```python
import math
import jax
import jax.numpy as jnp
from jax import lax

D = 8192
MODES = 16
CLIP_NORM = 512
SEQ = 1024


def draw_log_rate(key, part):
    pick_key, slow_key, fast_key = jax.random.split(jax.random.fold_in(key, 7), 3)
    top_rate = math.log(math.log(10.0) / SEQ)
    slow_rates = jax.random.uniform(slow_key, (D, MODES), jnp.float32, top_rate - math.log(10.0), top_rate)
    fast_rates = jax.random.uniform(fast_key, (D, MODES), jnp.float32, top_rate, -3.0)
    slow_share = 0.5
    chosen = jax.random.uniform(pick_key, (D, MODES), jnp.float32) < slow_share
    return jnp.where(chosen, slow_rates, fast_rates).astype(jnp.float32)


def draw_grad_out(key, part):
    level_key, base_key = jax.random.split(jax.random.fold_in(key, 13), 2)
    channel = jnp.arange(D, dtype=jnp.float32)
    levels = jax.random.uniform(level_key, (D,), jnp.float32, 0.0, 1.0)
    base_draw = jax.random.truncated_normal(base_key, -4.0, 4.0, (SEQ, D), jnp.float32)
    channel_scale = jnp.exp(levels * math.log(10.0) + channel / (D - 1) * math.log(3.0)) / 3.0
    return (base_draw * channel_scale[None, :]).astype(jnp.bfloat16)


def shard_levels(own_key, shape, pieces, low, largest):
    gain = 1.0
    for axis_at, parts in pieces:
        draws = jax.random.uniform(jax.random.fold_in(jax.random.fold_in(own_key, 6), axis_at), (parts,), jnp.float32, low / len(pieces), largest / len(pieces))
        gain = gain * jnp.repeat(jnp.exp(draws), shape[axis_at] // parts).reshape((-1,) + (1,) * (len(shape) - 1 - axis_at))
    return gain


def centred(stream_key, extent, spread, limit, cuts=(), held_as=jnp.bfloat16):
    level = shard_levels(stream_key, extent, cuts, -0.22, 0.18) if cuts else 1.0
    drawn = jax.random.normal(stream_key, extent, jnp.float32) * spread * level
    return jnp.minimum(jnp.maximum(drawn, -limit), limit).astype(held_as)


def setup_inputs(seed: int = 0) -> dict:
    key_of = jax.random.split(jax.random.key(seed), 7)
    grad_out = draw_grad_out(jax.random.fold_in(key_of[6], 71), 0)
    query_in = centred(key_of[1], (SEQ, D), 1.0, 6.0, ((0, 8), (1, 4)))
    key_in = centred(key_of[2], (SEQ, D), 1.0, 6.0, ((0, 8), (1, 4)))
    value_in = centred(key_of[3], (SEQ, D), 1.0, 6.0, ((0, 8), (1, 4)))
    residue = centred(key_of[4], (D, MODES), 0.25, 4.0, ((0, 4),), jnp.float32)
    log_rate = draw_log_rate(jax.random.fold_in(key_of[6], 71), 0)
    return {"grad_out": grad_out, "query_in": query_in, "key_in": key_in, "value_in": value_in, "residue": residue, "log_rate": log_rate}


def reference(grad_out, query_in, key_in, value_in, residue, log_rate):
    decay_rate = jnp.exp(log_rate)
    decay_step = jnp.exp(-decay_rate)
    mode_weight = residue * jnp.sqrt(2.0 * decay_rate)
    product = key_in.astype(jnp.float32) * value_in.astype(jnp.float32)
    gated_grad = grad_out.astype(jnp.float32) * query_in.astype(jnp.float32)
    zero_state = jnp.zeros(residue.shape, jnp.float32)

    def forward_step(carried, inputs_row):
        states, lagged, weight_sum, lag_total = carried
        product_row, gated_row = inputs_row
        lagged = decay_step * (lagged + states)
        states = decay_step * states + product_row[:, None]
        weight_sum = weight_sum + gated_row[:, None] * states
        lag_total = lag_total + gated_row[:, None] * lagged
        return ((states, lagged, weight_sum, lag_total), lax.optimization_barrier(jnp.sum(mode_weight * states, axis=1)))
    start_value = (zero_state, zero_state, zero_state, zero_state)
    finals, filtered = lax.scan(forward_step, start_value, (product, gated_grad))
    raw_weight = finals[2]
    lag_total = finals[3]

    def backward_step(adjoint, gated_row):
        adjoint = decay_step * adjoint + gated_row[:, None]
        return (adjoint, lax.optimization_barrier(jnp.sum(mode_weight * adjoint, axis=1)))
    _, back_filtered = lax.scan(backward_step, zero_state, gated_grad, reverse=True)
    grad_query = (grad_out.astype(jnp.float32) * filtered).astype(jnp.bfloat16)
    grad_key = (back_filtered * value_in.astype(jnp.float32)).astype(jnp.bfloat16)
    grad_value = (back_filtered * key_in.astype(jnp.float32)).astype(jnp.bfloat16)
    raw_residue = jnp.sqrt(2.0 * decay_rate) * raw_weight
    raw_rate = mode_weight * (0.5 * raw_weight - decay_rate * lag_total)
    squares = jnp.sum(raw_residue * raw_residue) + jnp.sum(raw_rate * raw_rate)
    grad_scale = jnp.minimum(1.0, CLIP_NORM / jnp.sqrt(squares + 1e-06))
    return (grad_query, grad_key, grad_value, raw_residue * grad_scale, raw_rate * grad_scale)
```

```python
import functools

import jax
import jax.numpy as jnp
from jax import lax
from jax.experimental import pallas as pl
from jax.experimental.pallas import tpu as pltpu
from jax.sharding import PartitionSpec as P

CLIP_NORM = 512
SUB = 8
LANES = 128
MESH = pl.DeviceIdType.MESH
VMEM_BYTES = 56 * 1024 * 1024


def shifted(x, by, row):
    moved = pltpu.roll(x, by % SUB, 0)
    keep = row >= by if by > 0 else row < SUB + by
    return jnp.where(keep, moved, 0.0)


def ends_kernel(rows, modes, go_ref, q_ref, k_ref, v_ref, lr_ref, ea_ref, sp_ref, an_ref, p_s, g_s):
    span = rows // SUB
    chunks = go_ref.shape[1] // LANES
    row = lax.broadcasted_iota(jnp.int32, (SUB, LANES), 0)

    def chunk(c, _):
        at = pl.ds(pl.multiple_of(c * LANES, LANES), LANES)
        p_s[...] = k_ref[:, at].astype(jnp.float32) * v_ref[:, at].astype(jnp.float32)
        g_s[...] = go_ref[:, at].astype(jnp.float32) * q_ref[:, at].astype(jnp.float32)
        rate = jnp.exp(lr_ref[:, at])
        decay = jnp.exp(-rate)
        steps = [jnp.exp(-rate * (span * n)) for n in (1, 2, 4)]
        for first in range(0, modes, 8):
            group = range(first, min(modes, first + 8))
            a = [jnp.broadcast_to(decay[m : m + 1], (SUB, LANES)) for m in group]
            s = [jnp.zeros((SUB, LANES), jnp.float32)] * len(a)
            for i in range(span):
                x = p_s[pl.ds(i, SUB, stride=span), :]
                s = [aa * ss + x for aa, ss in zip(a, s)]
            t = [jnp.zeros((SUB, LANES), jnp.float32)] * len(a)
            for i in reversed(range(span)):
                x = g_s[pl.ds(i, SUB, stride=span), :]
                t = [aa * tt + x for aa, tt in zip(a, t)]
            for at_m, m in enumerate(group):
                x, y = s[at_m], t[at_m]
                for n, table in zip((1, 2, 4), steps):
                    power = jnp.broadcast_to(table[m : m + 1], (SUB, LANES))
                    x = x + power * shifted(x, n, row)
                    y = y + power * shifted(y, -n, row)
                sp_ref[m, :, at] = shifted(x, 1, row)
                an_ref[m, :, at] = shifted(y, -1, row)
                ea_ref[0, m : m + 1, at] = x[SUB - 1 : SUB]
                ea_ref[1, m : m + 1, at] = y[0:1]
        return 0

    lax.fori_loop(0, chunks, chunk, 0)


def carry_kernel(n, rows, ea_ref, lr_ref, out_ref, held, send_sem, recv_sem):
    me = lax.axis_index("ctx")
    barrier = pltpu.get_barrier_semaphore()
    for k in range(1, n):
        pl.semaphore_signal(
            barrier, inc=1, device_id={"ctx": lax.rem(me + k, n)}, device_id_type=MESH
        )
    pl.semaphore_wait(barrier, n - 1)
    copies = []
    for k in range(1, n):
        there = lax.rem(me + k, n)
        which = jnp.where(there < me, 1, 0)
        copy = pltpu.make_async_remote_copy(
            src_ref=ea_ref.at[which],
            dst_ref=held.at[k - 1],
            send_sem=send_sem.at[k - 1],
            recv_sem=recv_sem.at[k - 1],
            device_id={"ctx": there},
            device_id_type=MESH,
        )
        copy.start()
        copies.append(copy)
    rate = jnp.exp(lr_ref[...])
    out_ref[...] = jnp.zeros_like(out_ref)
    for k in range(1, n):
        copies[k - 1].wait_recv()
        origin = lax.rem(me - k + n, n)
        which = jnp.where(origin < me, 0, 1)
        gap = jnp.where(origin < me, me - origin, origin - me) - 1
        power = jnp.exp(-rate * (gap * rows).astype(jnp.float32))
        out_ref[which] += power * held[k - 1]
    for copy in copies:
        copy.wait_send()


def main_kernel(
    rows, modes, go_ref, q_ref, k_ref, v_ref, lr_ref, res_ref, ca_ref, sp_ref, an_ref,
    gq_ref, gk_ref, gv_ref, w_ref, p_s, g_s, f_s, b_s, s_s, fr_s, br_s,
):
    span = rows // SUB
    chunks = go_ref.shape[1] // LANES
    row = lax.broadcasted_iota(jnp.int32, (SUB, LANES), 0).astype(jnp.float32)
    size = 4

    def chunk(c, _):
        at = pl.ds(pl.multiple_of(c * LANES, LANES), LANES)
        p_s[...] = k_ref[:, at].astype(jnp.float32) * v_ref[:, at].astype(jnp.float32)
        g_s[...] = go_ref[:, at].astype(jnp.float32) * q_ref[:, at].astype(jnp.float32)
        rate = jnp.exp(lr_ref[:, at])
        decay = jnp.exp(-rate)
        root = jnp.sqrt(2.0 * rate)
        weight = res_ref[:, at] * root
        carry_in = ca_ref[0, :, at]
        carry_back = ca_ref[1, :, at]
        wide = lambda x, m: jnp.broadcast_to(x[m : m + 1], (SUB, LANES))
        raw, lag = [], []
        for first in range(0, modes, size):
            group = range(first, first + size)
            a = [wide(decay, m) for m in group]
            w = [wide(weight, m) for m in group]
            s = [
                sp_ref[m, :, at] + jnp.exp(-wide(rate, m) * (span * row)) * wide(carry_in, m)
                for m in group
            ]
            t = [
                an_ref[m, :, at]
                + jnp.exp(-wide(rate, m) * (span * (SUB - 1 - row))) * wide(carry_back, m)
                for m in group
            ]
            rw = [jnp.zeros((SUB, LANES), jnp.float32)] * size
            lg = [jnp.zeros((SUB, LANES), jnp.float32)] * size
            for i in range(span):
                x = p_s[pl.ds(i, SUB, stride=span), :]
                y = g_s[pl.ds(i, SUB, stride=span), :]
                s = [aa * ss + x for aa, ss in zip(a, s)]
                for j in range(size):
                    s_s[i * size + j] = s[j]
                rw = [r + y * ss for r, ss in zip(rw, s)]
                f = (w[0] * s[0] + w[1] * s[1]) + (w[2] * s[2] + w[3] * s[3])
                if first == 0:
                    f_s[i] = f
                elif first + size < modes:
                    f_s[i] += f
                else:
                    fr_s[pl.ds(i, SUB, stride=span), :] = f_s[i] + f
            for i in reversed(range(span)):
                y = g_s[pl.ds(i, SUB, stride=span), :]
                lg = [l + s_s[i * size + j] * t[j] for j, l in enumerate(lg)]
                t = [aa * tt + y for aa, tt in zip(a, t)]
                b = (w[0] * t[0] + w[1] * t[1]) + (w[2] * t[2] + w[3] * t[3])
                if first == 0:
                    b_s[i] = b
                elif first + size < modes:
                    b_s[i] += b
                else:
                    br_s[pl.ds(i, SUB, stride=span), :] = b_s[i] + b
            raw += [jnp.sum(r, axis=0, keepdims=True) for r in rw]
            lag += [jnp.sum(l, axis=0, keepdims=True) for l in lg]
        gq_ref[:, at] = (go_ref[:, at].astype(jnp.float32) * fr_s[...]).astype(jnp.bfloat16)
        back = br_s[...]
        gk_ref[:, at] = (back * v_ref[:, at].astype(jnp.float32)).astype(jnp.bfloat16)
        gv_ref[:, at] = (back * k_ref[:, at].astype(jnp.float32)).astype(jnp.bfloat16)
        raw_weight = jnp.concatenate(raw, axis=0)
        lag_total = decay * jnp.concatenate(lag, axis=0)
        w_ref[c, 0:modes] = root * raw_weight
        w_ref[c, modes : 2 * modes] = weight * (0.5 * raw_weight - rate * lag_total)
        return 0

    lax.fori_loop(0, chunks, chunk, 0)


def clip_kernel(n, ntp, g_ref, out_ref, held, red, gath, squares, send_sem, recv_sem, sq_send, sq_recv):
    me = lax.axis_index("ctx")
    lane = lax.axis_index("tp")
    total = n * ntp
    here = me * ntp + lane
    tiles = g_ref.shape[0] // n
    barrier = pltpu.get_barrier_semaphore()

    def place(q):
        other = lax.rem(here + q, total)
        return {"ctx": other // ntp, "tp": lax.rem(other, ntp)}

    def greet(q, _):
        pl.semaphore_signal(barrier, inc=1, device_id=place(q), device_id_type=MESH)
        return 0

    lax.fori_loop(1, total, greet, 0)
    pl.semaphore_wait(barrier, total - 1)

    def send(phase, src, dst, k):
        copy = pltpu.make_async_remote_copy(
            src_ref=src,
            dst_ref=dst,
            send_sem=send_sem.at[phase, k - 1],
            recv_sem=recv_sem.at[phase, k - 1],
            device_id={"ctx": lax.rem(me + k, n)},
            device_id_type=MESH,
        )
        copy.start()
        return copy

    first = []
    for k in range(1, n):
        there = lax.rem(me + k, n)
        first.append(send(0, g_ref.at[pl.ds(there * tiles, tiles)], held.at[k - 1], k))
    mine = g_ref[pl.ds(me * tiles, tiles)]
    for k in range(1, n):
        first[k - 1].wait_recv()
        mine = mine + held[k - 1]
    red[...] = mine
    squares[here] = jnp.sum(mine * mine, axis=0)

    def sq_copy(q):
        return pltpu.make_async_remote_copy(
            src_ref=squares.at[here],
            dst_ref=squares.at[here],
            send_sem=sq_send.at[q - 1],
            recv_sem=sq_recv.at[q - 1],
            device_id=place(q),
            device_id_type=MESH,
        )

    def sq_start(q, _):
        sq_copy(q).start()
        return 0

    lax.fori_loop(1, total, sq_start, 0)
    second = [send(1, red, gath.at[pl.ds(me * tiles, tiles)], k) for k in range(1, n)]
    gath[pl.ds(me * tiles, tiles)] = mine

    def sq_wait(q, _):
        sq_copy(q).wait()
        return 0

    lax.fori_loop(1, total, sq_wait, 0)
    norm = jnp.sum(jnp.sum(squares[...], axis=0), keepdims=True)
    scale = jnp.minimum(1.0, CLIP_NORM / jnp.sqrt(norm + 1e-06))
    for copy in second:
        copy.wait_recv()
    out_ref[...] = gath[...] * scale
    for copy in first + second:
        copy.wait_send()


def per_device(n, ntp, grad_out, query_in, key_in, value_in, residue, log_rate):
    rows, chans = grad_out.shape
    modes = residue.shape[1]
    span = rows // SUB
    chunks = chans // LANES
    f32 = jnp.float32
    shape = jax.ShapeDtypeStruct
    vmem = pl.BlockSpec(memory_space=pltpu.VMEM)
    rate_t = log_rate.T
    res_t = residue.T
    data = (grad_out, query_in, key_in, value_in)
    tile = lambda *lead: pltpu.VMEM((*lead, SUB, LANES), f32)
    flat = pltpu.VMEM((rows, LANES), f32)
    ends, sprev, anext = pl.pallas_call(
        functools.partial(ends_kernel, rows, modes),
        out_shape=(
            shape((2, modes, chans), f32),
            shape((modes, SUB, chans), f32),
            shape((modes, SUB, chans), f32),
        ),
        in_specs=[vmem] * 5,
        out_specs=(vmem,) * 3,
        scratch_shapes=[flat, flat],
        compiler_params=pltpu.CompilerParams(vmem_limit_bytes=VMEM_BYTES),
        name="ends",
    )(*data, rate_t)
    carries = pl.pallas_call(
        functools.partial(carry_kernel, n, rows),
        out_shape=shape((2, modes, chans), f32),
        in_specs=[vmem] * 2,
        out_specs=vmem,
        scratch_shapes=[
            pltpu.VMEM((n - 1, modes, chans), f32),
            pltpu.SemaphoreType.DMA((n - 1,)),
            pltpu.SemaphoreType.DMA((n - 1,)),
        ],
        compiler_params=pltpu.CompilerParams(
            collective_id=0, has_side_effects=True, vmem_limit_bytes=VMEM_BYTES
        ),
        name="carry",
    )(ends, rate_t)
    grad_query, grad_key, grad_value, raw = pl.pallas_call(
        functools.partial(main_kernel, rows, modes),
        out_shape=(shape((rows, chans), jnp.bfloat16),) * 3
        + (shape((chunks, 2 * modes, LANES), f32),),
        in_specs=[vmem] * 9,
        out_specs=(vmem,) * 4,
        scratch_shapes=[flat, flat, tile(span), tile(span), tile(4 * span), flat, flat],
        compiler_params=pltpu.CompilerParams(vmem_limit_bytes=VMEM_BYTES),
        name="main",
    )(*data, rate_t, res_t, carries, sprev, anext)
    used = chunks * 2 * modes // SUB
    count = -(-used // n) * n
    raw = raw.reshape(used, SUB, LANES)
    if count > used:
        raw = jnp.pad(raw, ((0, count - used), (0, 0), (0, 0)))
    clipped = pl.pallas_call(
        functools.partial(clip_kernel, n, ntp),
        out_shape=shape((count, SUB, LANES), f32),
        in_specs=[vmem],
        out_specs=vmem,
        scratch_shapes=[
            tile(n - 1, count // n),
            tile(count // n),
            tile(count),
            tile(n * ntp),
            pltpu.SemaphoreType.DMA((2, n - 1)),
            pltpu.SemaphoreType.DMA((2, n - 1)),
            pltpu.SemaphoreType.DMA((n * ntp - 1,)),
            pltpu.SemaphoreType.DMA((n * ntp - 1,)),
        ],
        compiler_params=pltpu.CompilerParams(
            collective_id=1, has_side_effects=True, vmem_limit_bytes=VMEM_BYTES
        ),
        name="clip",
    )(raw)
    grads = clipped[:used].reshape(chunks, 2, modes, LANES).transpose(1, 0, 3, 2)
    grads = grads.reshape(2, chans, modes)
    return grad_query, grad_key, grad_value, grads[0], grads[1]


def solution(mesh):
    wide = P("ctx", "tp")
    tall = P("tp", None)
    body = functools.partial(per_device, mesh.shape["ctx"], mesh.shape["tp"])
    return jax.shard_map(
        body,
        mesh=mesh,
        in_specs=(wide,) * 4 + (tall,) * 2,
        out_specs=(wide,) * 3 + (tall,) * 2,
        check_vma=False,
    )
```

```python
import functools

import jax
import jax.numpy as jnp
from jax import lax
from jax.experimental import pallas as pl
from jax.experimental.pallas import tpu as pltpu
from jax.sharding import PartitionSpec as P

CLIP_NORM = 512
SUB = 8
LANES = 128
MESH = pl.DeviceIdType.MESH
VMEM_BYTES = 56 * 1024 * 1024


def shifted(x, by, row):
    moved = pltpu.roll(x, by % SUB, 0)
    keep = row >= by if by > 0 else row < SUB + by
    return jnp.where(keep, moved, 0.0)


def fused_kernel(
    n, ntp, modes, groups,
    go_ref, q_ref, k_ref, v_ref, lr_ref, res_ref,
    gq_ref, gk_ref, gv_ref, dres_ref, drate_ref,
    p_s, g_s, f_s, b_s, s_s, fr_s, br_s, sp_s, an_s,
    ea_s, held, ca_s, raw_s, parts, red, gath, squares,
    ex_send, ex_recv, rs_send, rs_recv, ag_send, ag_recv, sq_send, sq_recv,
):
    me = lax.axis_index("ctx")
    total = n * ntp
    here = me * ntp + lax.axis_index("tp")
    rows, chans = go_ref.shape
    span = rows // SUB
    per_group = chans // groups // LANES
    pieces = 2 * modes // SUB
    own = raw_s.shape[1] // n
    row = lax.broadcasted_iota(jnp.int32, (SUB, LANES), 0)
    level = row.astype(jnp.float32)
    zero = jnp.zeros((SUB, LANES), jnp.float32)
    size = 4

    def place(q):
        other = lax.rem(here + q, total)
        return {"ctx": other // ntp, "tp": lax.rem(other, ntp)}

    def peer(k):
        return {"ctx": lax.rem(me + k, n)}

    barrier = pltpu.get_barrier_semaphore()

    def greet(q, _):
        pl.semaphore_signal(barrier, inc=1, device_id=place(q), device_id_type=MESH)
        return 0

    lax.fori_loop(1, total, greet, 0)

    def wide(x, m):
        return jnp.broadcast_to(x[m : m + 1], (SUB, LANES))

    def gates(at):
        p_s[...] = k_ref[:, at].astype(jnp.float32) * v_ref[:, at].astype(jnp.float32)
        g_s[...] = go_ref[:, at].astype(jnp.float32) * q_ref[:, at].astype(jnp.float32)

    def places(g, c):
        at = pl.ds(pl.multiple_of((g * per_group + c) * LANES, LANES), LANES)
        return at, pl.ds(pl.multiple_of(c * LANES, LANES), LANES)

    def ends(g):
        def chunk(c, _):
            at, inner = places(g, c)
            gates(at)
            rate = jnp.exp(lr_ref[:, at])
            decay = jnp.exp(-rate)
            steps = [jnp.exp(-rate * (span * far)) for far in (1, 2, 4)]
            for first in range(0, modes, 8):
                group = range(first, min(modes, first + 8))
                a = [wide(decay, m) for m in group]
                s = [zero] * len(a)
                for i in range(span):
                    x = p_s[pl.ds(i, SUB, stride=span), :]
                    s = [aa * ss + x for aa, ss in zip(a, s)]
                t = [zero] * len(a)
                for i in reversed(range(span)):
                    x = g_s[pl.ds(i, SUB, stride=span), :]
                    t = [aa * tt + x for aa, tt in zip(a, t)]
                for slot, m in enumerate(group):
                    x, y = s[slot], t[slot]
                    for far, table in zip((1, 2, 4), steps):
                        power = wide(table, m)
                        x = x + power * shifted(x, far, row)
                        y = y + power * shifted(y, -far, row)
                    sp_s[m, :, at] = shifted(x, 1, row)
                    an_s[m, :, at] = shifted(y, -1, row)
                    ea_s[g, 0, m : m + 1, inner] = x[SUB - 1 : SUB]
                    ea_s[g, 1, m : m + 1, inner] = y[0:1]
            return 0

        lax.fori_loop(0, per_group, chunk, 0)

    def exchange(g, k):
        which = jnp.where(lax.rem(me + k, n) < me, 1, 0)
        return pltpu.make_async_remote_copy(
            src_ref=ea_s.at[g, which],
            dst_ref=held.at[g, k - 1],
            send_sem=ex_send.at[g, k - 1],
            recv_sem=ex_recv.at[g, k - 1],
            device_id=peer(k),
            device_id_type=MESH,
        )

    def scatter(g, k):
        there = lax.rem(me + k, n)
        return pltpu.make_async_remote_copy(
            src_ref=raw_s.at[g, pl.ds(there * own, own)],
            dst_ref=parts.at[g, k - 1],
            send_sem=rs_send.at[g, k - 1],
            recv_sem=rs_recv.at[g, k - 1],
            device_id=peer(k),
            device_id_type=MESH,
        )

    def gather(k):
        return pltpu.make_async_remote_copy(
            src_ref=red,
            dst_ref=gath.at[me],
            send_sem=ag_send.at[k - 1],
            recv_sem=ag_recv.at[k - 1],
            device_id=peer(k),
            device_id_type=MESH,
        )

    def norm(q):
        return pltpu.make_async_remote_copy(
            src_ref=squares.at[here],
            dst_ref=squares.at[here],
            send_sem=sq_send.at[q - 1],
            recv_sem=sq_recv.at[q - 1],
            device_id=place(q),
            device_id_type=MESH,
        )

    def carry(g):
        at = pl.ds(pl.multiple_of(g * per_group * LANES, LANES), per_group * LANES)
        rate = jnp.exp(lr_ref[:, at])
        ca_s[...] = jnp.zeros_like(ca_s)
        for k in range(1, n):
            exchange(g, k).wait_recv()
            origin = lax.rem(me - k + n, n)
            which = jnp.where(origin < me, 0, 1)
            gap = jnp.where(origin < me, me - origin, origin - me) - 1
            power = jnp.exp(-rate * (gap * rows).astype(jnp.float32))
            ca_s[which] += power * held[g, k - 1]

    def main(g):
        def chunk(c, _):
            at, inner = places(g, c)
            gates(at)
            rate = jnp.exp(lr_ref[:, at])
            decay = jnp.exp(-rate)
            root = jnp.sqrt(2.0 * rate)
            weight = res_ref[:, at] * root
            carry_in = ca_s[0, :, inner]
            carry_back = ca_s[1, :, inner]
            raw, lag = [], []
            for first in range(0, modes, size):
                group = range(first, first + size)
                a = [wide(decay, m) for m in group]
                w = [wide(weight, m) for m in group]
                s = [
                    sp_s[m, :, at]
                    + jnp.exp(-wide(rate, m) * (span * level)) * wide(carry_in, m)
                    for m in group
                ]
                t = [
                    an_s[m, :, at]
                    + jnp.exp(-wide(rate, m) * (span * (SUB - 1 - level))) * wide(carry_back, m)
                    for m in group
                ]
                rw = [zero] * size
                lg = [zero] * size
                for i in range(span):
                    x = p_s[pl.ds(i, SUB, stride=span), :]
                    y = g_s[pl.ds(i, SUB, stride=span), :]
                    s = [aa * ss + x for aa, ss in zip(a, s)]
                    for j in range(size):
                        s_s[i * size + j] = s[j]
                    rw = [r + y * ss for r, ss in zip(rw, s)]
                    f = (w[0] * s[0] + w[1] * s[1]) + (w[2] * s[2] + w[3] * s[3])
                    if first == 0:
                        f_s[i] = f
                    elif first + size < modes:
                        f_s[i] += f
                    else:
                        fr_s[pl.ds(i, SUB, stride=span), :] = f_s[i] + f
                for i in reversed(range(span)):
                    y = g_s[pl.ds(i, SUB, stride=span), :]
                    lg = [l + s_s[i * size + j] * t[j] for j, l in enumerate(lg)]
                    t = [aa * tt + y for aa, tt in zip(a, t)]
                    b = (w[0] * t[0] + w[1] * t[1]) + (w[2] * t[2] + w[3] * t[3])
                    if first == 0:
                        b_s[i] = b
                    elif first + size < modes:
                        b_s[i] += b
                    else:
                        br_s[pl.ds(i, SUB, stride=span), :] = b_s[i] + b
                raw += [jnp.sum(r, axis=0, keepdims=True) for r in rw]
                lag += [jnp.sum(l, axis=0, keepdims=True) for l in lg]
            gq_ref[:, at] = (go_ref[:, at].astype(jnp.float32) * fr_s[...]).astype(jnp.bfloat16)
            back = br_s[...]
            gk_ref[:, at] = (back * v_ref[:, at].astype(jnp.float32)).astype(jnp.bfloat16)
            gv_ref[:, at] = (back * k_ref[:, at].astype(jnp.float32)).astype(jnp.bfloat16)
            raw_weight = jnp.concatenate(raw, axis=0)
            lag_total = decay * jnp.concatenate(lag, axis=0)
            both = (root * raw_weight, weight * (0.5 * raw_weight - rate * lag_total))
            for piece in range(pieces):
                low = piece % (pieces // 2) * SUB
                raw_s[g, c * pieces + piece] = both[piece // (pieces // 2)][low : low + SUB]
            return 0

        lax.fori_loop(0, per_group, chunk, 0)

    if raw_s.shape[1] > per_group * pieces:
        raw_s[...] = jnp.zeros_like(raw_s)

    def first_stage(g, _):
        ends(g)
        for k in range(1, n):
            exchange(g, k).start()
        return 0

    def second_stage(g, _):
        carry(g)
        main(g)
        for k in range(1, n):
            scatter(g, k).start()
        return 0

    ends(0)
    pl.semaphore_wait(barrier, total - 1)
    for k in range(1, n):
        exchange(0, k).start()
    lax.fori_loop(1, groups, first_stage, 0)
    lax.fori_loop(0, groups, second_stage, 0)

    sums = zero
    for g in range(groups):
        mine = raw_s[g, pl.ds(me * own, own)]
        for k in range(1, n):
            scatter(g, k).wait_recv()
            mine = mine + parts[g, k - 1]
        red[g] = mine
        sums = sums + jnp.sum(mine * mine, axis=0)
    squares[here] = sums

    def norm_start(q, _):
        norm(q).start()
        return 0

    lax.fori_loop(1, total, norm_start, 0)
    for k in range(1, n):
        gather(k).start()
    gath[me] = red[...]

    def norm_wait(q, _):
        norm(q).wait()
        return 0

    lax.fori_loop(1, total, norm_wait, 0)
    square = jnp.sum(jnp.sum(squares[...], axis=0), keepdims=True)
    scale = jnp.minimum(1.0, CLIP_NORM / jnp.sqrt(square + 1e-06))
    for k in range(1, n):
        gather(k).wait_recv()
    for g in range(groups):
        for c in range(per_group):
            at = pl.ds((g * per_group + c) * LANES, LANES)
            for piece in range(pieces):
                tile = c * pieces + piece
                low = piece % (pieces // 2) * SUB
                ref = dres_ref if piece < pieces // 2 else drate_ref
                ref[low : low + SUB, at] = gath[tile // own, g, tile % own] * scale

    def drain(g, _):
        for k in range(1, n):
            exchange(g, k).wait_send()
            scatter(g, k).wait_send()
        return 0

    lax.fori_loop(0, groups, drain, 0)
    for k in range(1, n):
        gather(k).wait_send()


def per_device(n, ntp, grad_out, query_in, key_in, value_in, residue, log_rate):
    rows, chans = grad_out.shape
    modes = residue.shape[1]
    span = rows // SUB
    chunks = chans // LANES
    groups = 4 if chunks % 4 == 0 and n <= 32 else 1
    width = chans // groups
    own = -(-(width // LANES * 2 * modes // SUB) // n)
    f32 = jnp.float32
    shape = jax.ShapeDtypeStruct
    vmem = pl.BlockSpec(memory_space=pltpu.VMEM)
    buffer = lambda *dims: pltpu.VMEM(dims, f32)
    tile = lambda *lead: pltpu.VMEM((*lead, SUB, LANES), f32)
    flags = lambda *dims: pltpu.SemaphoreType.DMA(dims)
    flat = buffer(rows, LANES)
    wide_out = shape((rows, chans), jnp.bfloat16)
    tall_out = shape((modes, chans), f32)
    grad_query, grad_key, grad_value, d_res, d_rate = pl.pallas_call(
        functools.partial(fused_kernel, n, ntp, modes, groups),
        out_shape=(wide_out,) * 3 + (tall_out,) * 2,
        in_specs=[vmem] * 6,
        out_specs=(vmem,) * 5,
        scratch_shapes=[
            flat, flat, tile(span), tile(span), tile(4 * span), flat, flat,
            buffer(modes, SUB, chans),
            buffer(modes, SUB, chans),
            buffer(groups, 2, modes, width),
            buffer(groups, n - 1, modes, width),
            buffer(2, modes, width),
            tile(groups, own * n),
            tile(groups, n - 1, own),
            tile(groups, own),
            tile(n, groups, own),
            tile(n * ntp),
            flags(groups, n - 1), flags(groups, n - 1),
            flags(groups, n - 1), flags(groups, n - 1),
            flags(n - 1), flags(n - 1),
            flags(n * ntp - 1), flags(n * ntp - 1),
        ],
        compiler_params=pltpu.CompilerParams(
            collective_id=0, has_side_effects=True, vmem_limit_bytes=VMEM_BYTES
        ),
        name="fused",
    )(grad_out, query_in, key_in, value_in, log_rate.T, residue.T)
    return grad_query, grad_key, grad_value, d_res.T, d_rate.T


def solution(mesh):
    wide = P("ctx", "tp")
    tall = P("tp", None)
    body = functools.partial(per_device, mesh.shape["ctx"], mesh.shape["tp"])
    return jax.shard_map(
        body,
        mesh=mesh,
        in_specs=(wide,) * 4 + (tall,) * 2,
        out_specs=(wide,) * 3 + (tall,) * 2,
        check_vma=False,
    )
```

```python
import functools

import jax
import jax.numpy as jnp
from jax import lax
from jax.experimental import pallas as pl
from jax.experimental.pallas import tpu as pltpu
from jax.sharding import PartitionSpec as P

CLIP_NORM = 512
SUB = 8
LANES = 128
MESH = pl.DeviceIdType.MESH
VMEM_BYTES = 56 * 1024 * 1024


def shifted(x, by, row):
    moved = pltpu.roll(x, by % SUB, 0)
    keep = row >= by if by > 0 else row < SUB + by
    return jnp.where(keep, moved, 0.0)


def fused_kernel(
    n, ntp, modes, groups,
    go_ref, q_ref, k_ref, v_ref, lr_ref, res_ref,
    for_ref, back_ref, dres_ref, drate_ref, scale_ref,
    p_s, g_s, f_s, b_s, s_s, fr_s, br_s, sp_s, an_s,
    ea_s, mate, pt_s, held, ca_s, raw_s, parts, red, gath, squares,
    pa_send, pa_recv, ex_send, ex_recv, rs_send, rs_recv, ag_send, ag_recv, sq_send, sq_recv,
):
    me = lax.axis_index("ctx")
    pair = me // 2
    odd = lax.rem(me, 2)
    pairs = n // 2
    total = n * ntp
    here = me * ntp + lax.axis_index("tp")
    rows, chans = go_ref.shape
    span = rows // SUB
    per_group = chans // groups // LANES
    pieces = 2 * modes // SUB
    own = raw_s.shape[1] // n
    row = lax.broadcasted_iota(jnp.int32, (SUB, LANES), 0)
    level = row.astype(jnp.float32)
    zero = jnp.zeros((SUB, LANES), jnp.float32)
    size = 4

    def place(q):
        other = lax.rem(here + q, total)
        return {"ctx": other // ntp, "tp": lax.rem(other, ntp)}

    def peer(k):
        return {"ctx": lax.rem(me + k, n)}

    barrier = pltpu.get_barrier_semaphore()

    def greet(q, _):
        pl.semaphore_signal(barrier, inc=1, device_id=place(q), device_id_type=MESH)
        return 0

    lax.fori_loop(1, total, greet, 0)

    def wide(x, m):
        return jnp.broadcast_to(x[m : m + 1], (SUB, LANES))

    def gates(at):
        p_s[...] = k_ref[:, at].astype(jnp.float32) * v_ref[:, at].astype(jnp.float32)
        g_s[...] = go_ref[:, at].astype(jnp.float32) * q_ref[:, at].astype(jnp.float32)

    def places(g, c):
        at = pl.ds(pl.multiple_of((g * per_group + c) * LANES, LANES), LANES)
        return at, pl.ds(pl.multiple_of(c * LANES, LANES), LANES)

    def ends(g):
        def chunk(c, _):
            at, inner = places(g, c)
            gates(at)
            rate = jnp.exp(lr_ref[:, at])
            decay = jnp.exp(-rate)
            steps = [jnp.exp(-rate * (span * far)) for far in (1, 2, 4)]
            for first in range(0, modes, 8):
                group = range(first, min(modes, first + 8))
                a = [wide(decay, m) for m in group]
                s = [zero] * len(a)
                for i in range(span):
                    x = p_s[pl.ds(i, SUB, stride=span), :]
                    s = [aa * ss + x for aa, ss in zip(a, s)]
                t = [zero] * len(a)
                for i in reversed(range(span)):
                    x = g_s[pl.ds(i, SUB, stride=span), :]
                    t = [aa * tt + x for aa, tt in zip(a, t)]
                for slot, m in enumerate(group):
                    x, y = s[slot], t[slot]
                    for far, table in zip((1, 2, 4), steps):
                        power = wide(table, m)
                        x = x + power * shifted(x, far, row)
                        y = y + power * shifted(y, -far, row)
                    sp_s[m, :, at] = shifted(x, 1, row)
                    an_s[m, :, at] = shifted(y, -1, row)
                    ea_s[g, 0, m : m + 1, inner] = x[SUB - 1 : SUB]
                    ea_s[g, 1, m : m + 1, inner] = y[0:1]
            return 0

        lax.fori_loop(0, per_group, chunk, 0)

    def couple(g):
        return pltpu.make_async_remote_copy(
            src_ref=ea_s.at[g],
            dst_ref=mate.at[g],
            send_sem=pa_send.at[g],
            recv_sem=pa_recv.at[g],
            device_id={"ctx": pair * 2 + 1 - odd},
            device_id_type=MESH,
        )

    def exchange(g, k):
        there = lax.rem(pair + k, pairs)
        which = jnp.where(there < pair, 1, 0)
        return pltpu.make_async_remote_copy(
            src_ref=pt_s.at[g, which],
            dst_ref=held.at[g, k - 1],
            send_sem=ex_send.at[g, k - 1],
            recv_sem=ex_recv.at[g, k - 1],
            device_id={"ctx": there * 2 + odd},
            device_id_type=MESH,
        )

    def scatter(g, k):
        there = lax.rem(me + k, n)
        return pltpu.make_async_remote_copy(
            src_ref=raw_s.at[g, pl.ds(there * own, own)],
            dst_ref=parts.at[g, k - 1],
            send_sem=rs_send.at[g, k - 1],
            recv_sem=rs_recv.at[g, k - 1],
            device_id=peer(k),
            device_id_type=MESH,
        )

    def gather(k):
        return pltpu.make_async_remote_copy(
            src_ref=red,
            dst_ref=gath.at[me],
            send_sem=ag_send.at[k - 1],
            recv_sem=ag_recv.at[k - 1],
            device_id=peer(k),
            device_id_type=MESH,
        )

    def norm(q):
        return pltpu.make_async_remote_copy(
            src_ref=squares.at[here],
            dst_ref=squares.at[here],
            send_sem=sq_send.at[q - 1],
            recv_sem=sq_recv.at[q - 1],
            device_id=place(q),
            device_id_type=MESH,
        )

    def rates(g):
        at = pl.ds(pl.multiple_of(g * per_group * LANES, LANES), per_group * LANES)
        return jnp.exp(lr_ref[:, at])

    def join(g):
        couple(g).wait_recv()
        across = jnp.exp(-rates(g) * rows)
        mine, other = ea_s[g], mate[g]
        early = jnp.where(odd == 1, other, mine)
        late = jnp.where(odd == 1, mine, other)
        pt_s[g, 0] = across * early[0] + late[0]
        pt_s[g, 1] = early[1] + across * late[1]
        for k in range(1, pairs):
            exchange(g, k).start()

    def carry(g):
        rate = rates(g)
        ca_s[...] = jnp.zeros_like(ca_s)
        for k in range(1, pairs):
            exchange(g, k).wait_recv()
            origin = lax.rem(pair - k + pairs, pairs)
            which = jnp.where(origin < pair, 0, 1)
            gap = jnp.where(origin < pair, pair - origin, origin - pair) - 1
            power = jnp.exp(-rate * (gap * (2 * rows)).astype(jnp.float32))
            ca_s[which] += power * held[g, k - 1]
        near = 1 - odd
        ca_s[near] = mate[g, near] + jnp.exp(-rate * rows) * ca_s[near]

    def main(g):
        def chunk(c, _):
            at, inner = places(g, c)
            gates(at)
            rate = jnp.exp(lr_ref[:, at])
            decay = jnp.exp(-rate)
            root = jnp.sqrt(2.0 * rate)
            weight = res_ref[:, at] * root
            carry_in = ca_s[0, :, inner]
            carry_back = ca_s[1, :, inner]
            raw, lag = [], []
            for first in range(0, modes, size):
                group = range(first, first + size)
                a = [wide(decay, m) for m in group]
                w = [wide(weight, m) for m in group]
                s = [
                    sp_s[m, :, at]
                    + jnp.exp(-wide(rate, m) * (span * level)) * wide(carry_in, m)
                    for m in group
                ]
                t = [
                    an_s[m, :, at]
                    + jnp.exp(-wide(rate, m) * (span * (SUB - 1 - level))) * wide(carry_back, m)
                    for m in group
                ]
                rw = [zero] * size
                lg = [zero] * size
                for i in range(span):
                    x = p_s[pl.ds(i, SUB, stride=span), :]
                    y = g_s[pl.ds(i, SUB, stride=span), :]
                    s = [aa * ss + x for aa, ss in zip(a, s)]
                    for j in range(size):
                        s_s[i * size + j] = s[j]
                    rw = [r + y * ss for r, ss in zip(rw, s)]
                    f = (w[0] * s[0] + w[1] * s[1]) + (w[2] * s[2] + w[3] * s[3])
                    if first == 0:
                        f_s[i] = f
                    elif first + size < modes:
                        f_s[i] += f
                    else:
                        fr_s[pl.ds(i, SUB, stride=span), :] = f_s[i] + f
                for i in reversed(range(span)):
                    y = g_s[pl.ds(i, SUB, stride=span), :]
                    lg = [l + s_s[i * size + j] * t[j] for j, l in enumerate(lg)]
                    t = [aa * tt + y for aa, tt in zip(a, t)]
                    b = (w[0] * t[0] + w[1] * t[1]) + (w[2] * t[2] + w[3] * t[3])
                    if first == 0:
                        b_s[i] = b
                    elif first + size < modes:
                        b_s[i] += b
                    else:
                        br_s[pl.ds(i, SUB, stride=span), :] = b_s[i] + b
                raw += [jnp.sum(r, axis=0, keepdims=True) for r in rw]
                lag += [jnp.sum(l, axis=0, keepdims=True) for l in lg]
            for_ref[:, at] = fr_s[...]
            back_ref[:, at] = br_s[...]
            raw_weight = jnp.concatenate(raw, axis=0)
            lag_total = decay * jnp.concatenate(lag, axis=0)
            both = (root * raw_weight, weight * (0.5 * raw_weight - rate * lag_total))
            for piece in range(pieces):
                low = piece % (pieces // 2) * SUB
                raw_s[g, c * pieces + piece] = both[piece // (pieces // 2)][low : low + SUB]
            return 0

        lax.fori_loop(0, per_group, chunk, 0)

    if raw_s.shape[1] > per_group * pieces:
        raw_s[...] = jnp.zeros_like(raw_s)

    def first_stage(g, _):
        ends(g)
        couple(g).start()
        join(g - 1)
        return 0

    def second_stage(g, _):
        carry(g)
        main(g)
        for k in range(1, n):
            scatter(g, k).start()
        return 0

    ends(0)
    pl.semaphore_wait(barrier, total - 1)
    couple(0).start()
    lax.fori_loop(1, groups, first_stage, 0)
    join(groups - 1)
    lax.fori_loop(0, groups, second_stage, 0)

    sums = zero
    for g in range(groups):
        mine = raw_s[g, pl.ds(me * own, own)]
        for k in range(1, n):
            scatter(g, k).wait_recv()
            mine = mine + parts[g, k - 1]
        red[g] = mine
        sums = sums + jnp.sum(mine * mine, axis=0)
    squares[here] = sums

    def norm_start(q, _):
        norm(q).start()
        return 0

    for k in range(1, n):
        gather(k).start()
    lax.fori_loop(1, total, norm_start, 0)
    gath[me] = red[...]

    def norm_wait(q, _):
        norm(q).wait()
        return 0

    lax.fori_loop(1, total, norm_wait, 0)
    square = jnp.sum(jnp.sum(squares[...], axis=0), keepdims=True)
    scale = jnp.minimum(1.0, CLIP_NORM / jnp.sqrt(square + 1e-06))
    scale_ref[...] = jnp.broadcast_to(scale, (SUB, LANES))
    for k in range(1, n):
        gather(k).wait_recv()
    for g in range(groups):
        for c in range(per_group):
            at = pl.ds((g * per_group + c) * LANES, LANES)
            for piece in range(pieces):
                tile = c * pieces + piece
                low = piece % (pieces // 2) * SUB
                ref = dres_ref if piece < pieces // 2 else drate_ref
                ref[low : low + SUB, at] = gath[tile // own, g, tile % own]

    def drain(g, _):
        couple(g).wait_send()
        for k in range(1, pairs):
            exchange(g, k).wait_send()
        for k in range(1, n):
            scatter(g, k).wait_send()
        return 0

    lax.fori_loop(0, groups, drain, 0)
    for k in range(1, n):
        gather(k).wait_send()


def per_device(n, ntp, grad_out, query_in, key_in, value_in, residue, log_rate):
    rows, chans = grad_out.shape
    modes = residue.shape[1]
    span = rows // SUB
    chunks = chans // LANES
    groups = 4 if chunks % 4 == 0 and n <= 32 else 1
    width = chans // groups
    own = -(-(width // LANES * 2 * modes // SUB) // n)
    f32 = jnp.float32
    shape = jax.ShapeDtypeStruct
    vmem = pl.BlockSpec(memory_space=pltpu.VMEM)
    buffer = lambda *dims: pltpu.VMEM(dims, f32)
    tile = lambda *lead: pltpu.VMEM((*lead, SUB, LANES), f32)
    flags = lambda *dims: pltpu.SemaphoreType.DMA(dims)
    flat = buffer(rows, LANES)
    wide_out = shape((rows, chans), f32)
    tall_out = shape((modes, chans), f32)
    filtered, back_filtered, d_res, d_rate, scale = pl.pallas_call(
        functools.partial(fused_kernel, n, ntp, modes, groups),
        out_shape=(wide_out,) * 2 + (tall_out,) * 2 + (shape((SUB, LANES), f32),),
        in_specs=[vmem] * 6,
        out_specs=(vmem,) * 5,
        scratch_shapes=[
            flat, flat, tile(span), tile(span), tile(4 * span), flat, flat,
            buffer(modes, SUB, chans),
            buffer(modes, SUB, chans),
            buffer(groups, 2, modes, width),
            buffer(groups, 2, modes, width),
            buffer(groups, 2, modes, width),
            buffer(groups, n // 2 - 1, modes, width),
            buffer(2, modes, width),
            tile(groups, own * n),
            tile(groups, n - 1, own),
            tile(groups, own),
            tile(n, groups, own),
            tile(n * ntp),
            flags(groups), flags(groups),
            flags(groups, n // 2 - 1), flags(groups, n // 2 - 1),
            flags(groups, n - 1), flags(groups, n - 1),
            flags(n - 1), flags(n - 1),
            flags(n * ntp - 1), flags(n * ntp - 1),
        ],
        compiler_params=pltpu.CompilerParams(
            collective_id=0, has_side_effects=True, vmem_limit_bytes=VMEM_BYTES
        ),
        name="fused",
    )(grad_out, query_in, key_in, value_in, log_rate.T, residue.T)
    grad_query = (grad_out.astype(f32) * filtered).astype(jnp.bfloat16)
    grad_key = (back_filtered * value_in.astype(f32)).astype(jnp.bfloat16)
    grad_value = (back_filtered * key_in.astype(f32)).astype(jnp.bfloat16)
    factor = scale[0, 0]
    return grad_query, grad_key, grad_value, d_res.T * factor, d_rate.T * factor


def solution(mesh):
    wide = P("ctx", "tp")
    tall = P("tp", None)
    body = functools.partial(per_device, mesh.shape["ctx"], mesh.shape["tp"])
    return jax.shard_map(
        body,
        mesh=mesh,
        in_specs=(wide,) * 4 + (tall,) * 2,
        out_specs=(wide,) * 3 + (tall,) * 2,
        check_vma=False,
    )
```

```python
import functools

import jax
import jax.numpy as jnp
from jax import lax
from jax.experimental import pallas as pl
from jax.experimental.pallas import tpu as pltpu
from jax.sharding import PartitionSpec as P

CLIP_NORM = 512
SUB = 8
LANES = 128
MESH = pl.DeviceIdType.MESH
VMEM_BYTES = 56 * 1024 * 1024


def shifted(x, by, row):
    moved = pltpu.roll(x, by % SUB, 0)
    keep = row >= by if by > 0 else row < SUB + by
    return jnp.where(keep, moved, 0.0)


def total_of(terms):
    while len(terms) > 1:
        terms = [x + y for x, y in zip(terms[::2], terms[1::2])]
    return terms[0]


def fused_kernel(
    n, ntp, modes, groups,
    go_ref, q_ref, k_ref, v_ref, lr_ref, res_ref,
    for_ref, back_ref, dres_ref, drate_ref,
    p_s, g_s, f_s, b_s, s_s, fr_s, br_s, sp_s, an_s,
    ea_s, mate, pt_s, held, ca_s, raw_s, parts, red, gath, sums, squares,
    pa_send, pa_recv, ex_send, ex_recv, rs_send, rs_recv, ag_send, ag_recv, sq_send, sq_recv,
):
    me = lax.axis_index("ctx")
    pair = me // 2
    odd = lax.rem(me, 2)
    pairs = n // 2
    total = n * ntp
    here = me * ntp + lax.axis_index("tp")
    rows, chans = go_ref.shape
    span = rows // SUB
    per_group = chans // groups // LANES
    pieces = 2 * modes // SUB
    own = raw_s.shape[1] // n
    row = lax.broadcasted_iota(jnp.int32, (SUB, LANES), 0)
    level = row.astype(jnp.float32)
    zero = jnp.zeros((SUB, LANES), jnp.float32)
    size = 8

    def place(q):
        other = lax.rem(here + q, total)
        return {"ctx": other // ntp, "tp": lax.rem(other, ntp)}

    def peer(k):
        return {"ctx": lax.rem(me + k, n)}

    barrier = pltpu.get_barrier_semaphore()

    def greet(q, _):
        pl.semaphore_signal(barrier, inc=1, device_id=place(q), device_id_type=MESH)
        return 0

    lax.fori_loop(1, total, greet, 0)

    def wide(x, m):
        return jnp.broadcast_to(x[m : m + 1], (SUB, LANES))

    def gates(at):
        p_s[...] = k_ref[:, at].astype(jnp.float32) * v_ref[:, at].astype(jnp.float32)
        g_s[...] = go_ref[:, at].astype(jnp.float32) * q_ref[:, at].astype(jnp.float32)

    def places(g, c):
        at = pl.ds(pl.multiple_of((g * per_group + c) * LANES, LANES), LANES)
        return at, pl.ds(pl.multiple_of(c * LANES, LANES), LANES)

    def ends(g):
        def chunk(c, _):
            at, inner = places(g, c)
            gates(at)
            rate = jnp.exp(lr_ref[:, at])
            decay = jnp.exp(-rate)
            steps = [jnp.exp(-rate * (span * far)) for far in (1, 2, 4)]
            for first in range(0, modes, 8):
                group = range(first, min(modes, first + 8))
                a = [wide(decay, m) for m in group]
                s = [zero] * len(a)
                t = [zero] * len(a)
                for i in range(span):
                    x = p_s[pl.ds(i, SUB, stride=span), :]
                    y = g_s[pl.ds(span - 1 - i, SUB, stride=span), :]
                    s = [aa * ss + x for aa, ss in zip(a, s)]
                    t = [aa * tt + y for aa, tt in zip(a, t)]
                for slot, m in enumerate(group):
                    x, y = s[slot], t[slot]
                    for far, table in zip((1, 2, 4), steps):
                        power = wide(table, m)
                        x = x + power * shifted(x, far, row)
                        y = y + power * shifted(y, -far, row)
                    sp_s[m, :, at] = shifted(x, 1, row)
                    an_s[m, :, at] = shifted(y, -1, row)
                    ea_s[g, 0, m : m + 1, inner] = x[SUB - 1 : SUB]
                    ea_s[g, 1, m : m + 1, inner] = y[0:1]
            return 0

        lax.fori_loop(0, per_group, chunk, 0)

    def couple(g):
        return pltpu.make_async_remote_copy(
            src_ref=ea_s.at[g],
            dst_ref=mate.at[g],
            send_sem=pa_send.at[g],
            recv_sem=pa_recv.at[g],
            device_id={"ctx": pair * 2 + 1 - odd},
            device_id_type=MESH,
        )

    def exchange(g, k):
        there = lax.rem(pair + k, pairs)
        which = jnp.where(there < pair, 1, 0)
        return pltpu.make_async_remote_copy(
            src_ref=pt_s.at[g, which],
            dst_ref=held.at[g, k - 1],
            send_sem=ex_send.at[g, k - 1],
            recv_sem=ex_recv.at[g, k - 1],
            device_id={"ctx": there * 2 + odd},
            device_id_type=MESH,
        )

    def scatter(g, k):
        there = lax.rem(me + k, n)
        return pltpu.make_async_remote_copy(
            src_ref=raw_s.at[g, pl.ds(there * own, own)],
            dst_ref=parts.at[g, k - 1],
            send_sem=rs_send.at[g, k - 1],
            recv_sem=rs_recv.at[g, k - 1],
            device_id=peer(k),
            device_id_type=MESH,
        )

    def gather(g, k):
        return pltpu.make_async_remote_copy(
            src_ref=red.at[g],
            dst_ref=gath.at[g, me],
            send_sem=ag_send.at[g, k - 1],
            recv_sem=ag_recv.at[g, k - 1],
            device_id=peer(k),
            device_id_type=MESH,
        )

    def norm(q):
        return pltpu.make_async_remote_copy(
            src_ref=squares.at[here],
            dst_ref=squares.at[here],
            send_sem=sq_send.at[q - 1],
            recv_sem=sq_recv.at[q - 1],
            device_id=place(q),
            device_id_type=MESH,
        )

    def rates(g):
        at = pl.ds(pl.multiple_of(g * per_group * LANES, LANES), per_group * LANES)
        return jnp.exp(lr_ref[:, at])

    def join(g):
        couple(g).wait_recv()
        across = jnp.exp(-rates(g) * rows)
        mine, other = ea_s[g], mate[g]
        early = jnp.where(odd == 1, other, mine)
        late = jnp.where(odd == 1, mine, other)
        pt_s[g, 0] = across * early[0] + late[0]
        pt_s[g, 1] = early[1] + across * late[1]
        for k in range(1, pairs):
            exchange(g, k).start()

    def carry(g):
        rate = rates(g)
        ca_s[...] = jnp.zeros_like(ca_s)
        for k in range(1, pairs):
            exchange(g, k).wait_recv()
            origin = lax.rem(pair - k + pairs, pairs)
            which = jnp.where(origin < pair, 0, 1)
            gap = jnp.where(origin < pair, pair - origin, origin - pair) - 1
            power = jnp.exp(-rate * (gap * (2 * rows)).astype(jnp.float32))
            ca_s[which] += power * held[g, k - 1]
        near = 1 - odd
        ca_s[near] = mate[g, near] + jnp.exp(-rate * rows) * ca_s[near]

    def main(g):
        def chunk(c, _):
            at, inner = places(g, c)
            gates(at)
            rate = jnp.exp(lr_ref[:, at])
            decay = jnp.exp(-rate)
            root = jnp.sqrt(2.0 * rate)
            weight = res_ref[:, at] * root
            carry_in = ca_s[0, :, inner]
            carry_back = ca_s[1, :, inner]
            raw, lag = [], []
            for first in range(0, modes, size):
                group = range(first, first + size)
                a = [wide(decay, m) for m in group]
                w = [wide(weight, m) for m in group]
                s = [
                    sp_s[m, :, at]
                    + jnp.exp(-wide(rate, m) * (span * level)) * wide(carry_in, m)
                    for m in group
                ]
                t = [
                    an_s[m, :, at]
                    + jnp.exp(-wide(rate, m) * (span * (SUB - 1 - level))) * wide(carry_back, m)
                    for m in group
                ]
                rw = [zero] * size
                lg = [zero] * size
                for i in range(span):
                    x = p_s[pl.ds(i, SUB, stride=span), :]
                    y = g_s[pl.ds(i, SUB, stride=span), :]
                    s = [aa * ss + x for aa, ss in zip(a, s)]
                    for j in range(size):
                        s_s[i * size + j] = s[j]
                    rw = [r + y * ss for r, ss in zip(rw, s)]
                    f = total_of([ww * ss for ww, ss in zip(w, s)])
                    if first == 0:
                        f_s[i] = f
                    elif first + size < modes:
                        f_s[i] += f
                    else:
                        fr_s[pl.ds(i, SUB, stride=span), :] = f_s[i] + f
                for i in reversed(range(span)):
                    y = g_s[pl.ds(i, SUB, stride=span), :]
                    lg = [l + s_s[i * size + j] * t[j] for j, l in enumerate(lg)]
                    t = [aa * tt + y for aa, tt in zip(a, t)]
                    b = total_of([ww * tt for ww, tt in zip(w, t)])
                    if first == 0:
                        b_s[i] = b
                    elif first + size < modes:
                        b_s[i] += b
                    else:
                        br_s[pl.ds(i, SUB, stride=span), :] = b_s[i] + b
                raw += [jnp.sum(r, axis=0, keepdims=True) for r in rw]
                lag += [jnp.sum(l, axis=0, keepdims=True) for l in lg]
            for_ref[:, at] = fr_s[...]
            back_ref[:, at] = br_s[...]
            raw_weight = jnp.concatenate(raw, axis=0)
            lag_total = decay * jnp.concatenate(lag, axis=0)
            both = (root * raw_weight, weight * (0.5 * raw_weight - rate * lag_total))
            for piece in range(pieces):
                low = piece % (pieces // 2) * SUB
                raw_s[g, c * pieces + piece] = both[piece // (pieces // 2)][low : low + SUB]
            return 0

        lax.fori_loop(0, per_group, chunk, 0)

    if raw_s.shape[1] > per_group * pieces:
        raw_s[...] = jnp.zeros_like(raw_s)

    def first_stage(g, _):
        ends(g)
        couple(g).start()
        join(g - 1)
        return 0

    def produce(g):
        carry(g)
        main(g)
        for k in range(1, n):
            scatter(g, k).start()

    def finish(g):
        mine = raw_s[g, pl.ds(me * own, own)]
        for k in range(1, n):
            scatter(g, k).wait_recv()
            mine = mine + parts[g, k - 1]
        red[g] = mine
        for k in range(1, n):
            gather(g, k).start()
        gath[g, me] = mine
        sums[...] += jnp.sum(mine * mine, axis=0)

    def second_stage(g, _):
        produce(g)
        finish(g - 1)
        return 0

    sums[...] = zero
    ends(0)
    pl.semaphore_wait(barrier, total - 1)
    couple(0).start()
    lax.fori_loop(1, groups, first_stage, 0)
    if groups == 1:
        join(0)
    produce(0)
    if groups > 1:
        join(groups - 1)
    lax.fori_loop(1, groups, second_stage, 0)
    finish(groups - 1)
    squares[here] = sums[...]

    def norm_start(q, _):
        norm(q).start()
        return 0

    lax.fori_loop(1, total, norm_start, 0)

    def norm_wait(q, _):
        norm(q).wait()
        return 0

    lax.fori_loop(1, total, norm_wait, 0)
    square = jnp.sum(jnp.sum(squares[...], axis=0), keepdims=True)
    scale = jnp.minimum(1.0, CLIP_NORM / jnp.sqrt(square + 1e-06))
    for g in range(groups):
        for k in range(1, n):
            gather(g, k).wait_recv()
        for c in range(per_group):
            at = pl.ds((g * per_group + c) * LANES, LANES)
            for piece in range(pieces):
                tile = c * pieces + piece
                low = piece % (pieces // 2) * SUB
                ref = dres_ref if piece < pieces // 2 else drate_ref
                ref[low : low + SUB, at] = gath[g, tile // own, tile % own] * scale

    def drain(g, _):
        couple(g).wait_send()
        for k in range(1, pairs):
            exchange(g, k).wait_send()
        for k in range(1, n):
            scatter(g, k).wait_send()
            gather(g, k).wait_send()
        return 0

    lax.fori_loop(0, groups, drain, 0)

def per_device(n, ntp, grad_out, query_in, key_in, value_in, residue, log_rate):
    rows, chans = grad_out.shape
    modes = residue.shape[1]
    span = rows // SUB
    chunks = chans // LANES
    groups = 4 if chunks % 4 == 0 and n <= 32 else 1
    width = chans // groups
    own = -(-(width // LANES * 2 * modes // SUB) // n)
    f32 = jnp.float32
    shape = jax.ShapeDtypeStruct
    vmem = pl.BlockSpec(memory_space=pltpu.VMEM)
    buffer = lambda *dims: pltpu.VMEM(dims, f32)
    tile = lambda *lead: pltpu.VMEM((*lead, SUB, LANES), f32)
    flags = lambda *dims: pltpu.SemaphoreType.DMA(dims)
    flat = buffer(rows, LANES)
    wide_out = shape((rows, chans), f32)
    tall_out = shape((modes, chans), f32)
    filtered, back_filtered, d_res, d_rate = pl.pallas_call(
        functools.partial(fused_kernel, n, ntp, modes, groups),
        out_shape=(wide_out,) * 2 + (tall_out,) * 2,
        in_specs=[vmem] * 6,
        out_specs=(vmem,) * 4,
        scratch_shapes=[
            flat, flat, tile(span), tile(span), tile(8 * span), flat, flat,
            buffer(modes, SUB, chans),
            buffer(modes, SUB, chans),
            buffer(groups, 2, modes, width),
            buffer(groups, 2, modes, width),
            buffer(groups, 2, modes, width),
            buffer(groups, n // 2 - 1, modes, width),
            buffer(2, modes, width),
            tile(groups, own * n),
            tile(groups, n - 1, own),
            tile(groups, own),
            tile(groups, n, own),
            tile(),
            tile(n * ntp),
            flags(groups), flags(groups),
            flags(groups, n // 2 - 1), flags(groups, n // 2 - 1),
            flags(groups, n - 1), flags(groups, n - 1),
            flags(groups, n - 1), flags(groups, n - 1),
            flags(n * ntp - 1), flags(n * ntp - 1),
        ],
        compiler_params=pltpu.CompilerParams(
            collective_id=0, has_side_effects=True, vmem_limit_bytes=VMEM_BYTES
        ),
        name="fused",
    )(grad_out, query_in, key_in, value_in, log_rate.T, residue.T)
    grad_query = (grad_out.astype(f32) * filtered).astype(jnp.bfloat16)
    grad_key = (back_filtered * value_in.astype(f32)).astype(jnp.bfloat16)
    grad_value = (back_filtered * key_in.astype(f32)).astype(jnp.bfloat16)
    return grad_query, grad_key, grad_value, d_res.T, d_rate.T


def solution(mesh):
    wide = P("ctx", "tp")
    tall = P("tp", None)
    body = functools.partial(per_device, mesh.shape["ctx"], mesh.shape["tp"])
    return jax.shard_map(
        body,
        mesh=mesh,
        in_specs=(wide,) * 4 + (tall,) * 2,
        out_specs=(wide,) * 3 + (tall,) * 2,
        check_vma=False,
    )
```

```python
import functools

import jax
import jax.numpy as jnp
from jax import lax
from jax.experimental import pallas as pl
from jax.experimental.pallas import tpu as pltpu
from jax.sharding import PartitionSpec as P

CLIP_NORM = 512
SUB = 8
LANES = 128
MESH = pl.DeviceIdType.MESH
VMEM_BYTES = 56 * 1024 * 1024


def shifted(x, by, row):
    moved = pltpu.roll(x, by % SUB, 0)
    keep = row >= by if by > 0 else row < SUB + by
    return jnp.where(keep, moved, 0.0)


def total_of(terms):
    while len(terms) > 1:
        terms = [x + y for x, y in zip(terms[::2], terms[1::2])]
    return terms[0]


def fused_kernel(
    n, ntp, modes, groups,
    go_ref, q_ref, k_ref, v_ref, lr_ref, res_ref,
    for_ref, back_ref, dres_ref, drate_ref,
    p_s, g_s, f_s, b_s, s_s, fr_s, br_s, sp_s, an_s,
    ea_s, mate, pt_s, held, ca_s, raw_s, parts, red, gath, sums, squares,
    pa_send, pa_recv, ex_send, ex_recv, rs_send, rs_recv, ag_send, ag_recv, sq_send, sq_recv,
):
    me = lax.axis_index("ctx")
    pair = me // 2
    odd = lax.rem(me, 2)
    pairs = n // 2
    total = n * ntp
    here = me * ntp + lax.axis_index("tp")
    rows, chans = go_ref.shape
    span = rows // SUB
    per_group = chans // groups // LANES
    pieces = 2 * modes // SUB
    own = raw_s.shape[1] // n
    row = lax.broadcasted_iota(jnp.int32, (SUB, LANES), 0)
    level = row.astype(jnp.float32)
    zero = jnp.zeros((SUB, LANES), jnp.float32)
    size = 8

    def place(q):
        other = lax.rem(here + q, total)
        return {"ctx": other // ntp, "tp": lax.rem(other, ntp)}

    def peer(k):
        return {"ctx": lax.rem(me + k, n)}

    barrier = pltpu.get_barrier_semaphore()

    def greet(q, _):
        pl.semaphore_signal(barrier, inc=1, device_id=place(q), device_id_type=MESH)
        return 0

    lax.fori_loop(1, total, greet, 0)

    def wide(x, m):
        return jnp.broadcast_to(x[m : m + 1], (SUB, LANES))

    def gates(at):
        p_s[...] = k_ref[:, at].astype(jnp.float32) * v_ref[:, at].astype(jnp.float32)
        g_s[...] = go_ref[:, at].astype(jnp.float32) * q_ref[:, at].astype(jnp.float32)

    def places(g, c):
        at = pl.ds(pl.multiple_of((g * per_group + c) * LANES, LANES), LANES)
        return at, pl.ds(pl.multiple_of(c * LANES, LANES), LANES)

    def ends(g):
        def chunk(c, _):
            at, inner = places(g, c)
            gates(at)
            rate = jnp.exp(lr_ref[:, at])
            decay = jnp.exp(-rate)
            steps = [jnp.exp(-rate * (span * far)) for far in (1, 2, 4)]
            for first in range(0, modes, 8):
                group = range(first, min(modes, first + 8))
                a = [wide(decay, m) for m in group]
                s = [zero] * len(a)
                t = [zero] * len(a)
                for i in range(span):
                    x = p_s[pl.ds(i, SUB, stride=span), :]
                    y = g_s[pl.ds(span - 1 - i, SUB, stride=span), :]
                    s = [aa * ss + x for aa, ss in zip(a, s)]
                    t = [aa * tt + y for aa, tt in zip(a, t)]
                for slot, m in enumerate(group):
                    x, y = s[slot], t[slot]
                    for far, table in zip((1, 2, 4), steps):
                        power = wide(table, m)
                        x = x + power * shifted(x, far, row)
                        y = y + power * shifted(y, -far, row)
                    sp_s[m, :, at] = shifted(x, 1, row)
                    an_s[m, :, at] = shifted(y, -1, row)
                    ea_s[g, 0, m : m + 1, inner] = x[SUB - 1 : SUB]
                    ea_s[g, 1, m : m + 1, inner] = y[0:1]
            return 0

        lax.fori_loop(0, per_group, chunk, 0)

    def couple(g):
        return pltpu.make_async_remote_copy(
            src_ref=ea_s.at[g],
            dst_ref=mate.at[g],
            send_sem=pa_send.at[g],
            recv_sem=pa_recv.at[g],
            device_id={"ctx": pair * 2 + 1 - odd},
            device_id_type=MESH,
        )

    def exchange(g, k):
        there = lax.rem(pair + k, pairs)
        which = jnp.where(there < pair, 1, 0)
        return pltpu.make_async_remote_copy(
            src_ref=pt_s.at[g, which],
            dst_ref=held.at[g, k - 1],
            send_sem=ex_send.at[g, k - 1],
            recv_sem=ex_recv.at[g, k - 1],
            device_id={"ctx": there * 2 + odd},
            device_id_type=MESH,
        )

    def scatter(g, k):
        there = lax.rem(me + k, n)
        return pltpu.make_async_remote_copy(
            src_ref=raw_s.at[g, pl.ds(there * own, own)],
            dst_ref=parts.at[g, k - 1],
            send_sem=rs_send.at[g, k - 1],
            recv_sem=rs_recv.at[g, k - 1],
            device_id=peer(k),
            device_id_type=MESH,
        )

    def gather(g, k):
        return pltpu.make_async_remote_copy(
            src_ref=red.at[g],
            dst_ref=gath.at[g, me],
            send_sem=ag_send.at[g, k - 1],
            recv_sem=ag_recv.at[g, k - 1],
            device_id=peer(k),
            device_id_type=MESH,
        )

    def norm(q):
        return pltpu.make_async_remote_copy(
            src_ref=squares.at[here],
            dst_ref=squares.at[here],
            send_sem=sq_send.at[q - 1],
            recv_sem=sq_recv.at[q - 1],
            device_id=place(q),
            device_id_type=MESH,
        )

    def rates(g):
        at = pl.ds(pl.multiple_of(g * per_group * LANES, LANES), per_group * LANES)
        return jnp.exp(lr_ref[:, at])

    def join(g):
        couple(g).wait_recv()
        across = jnp.exp(-rates(g) * rows)
        mine, other = ea_s[g], mate[g]
        early = jnp.where(odd == 1, other, mine)
        late = jnp.where(odd == 1, mine, other)
        pt_s[g, 0] = across * early[0] + late[0]
        pt_s[g, 1] = early[1] + across * late[1]
        for k in range(1, pairs):
            exchange(g, k).start()

    def carry(g):
        rate = rates(g)
        ca_s[...] = jnp.zeros_like(ca_s)
        for k in range(1, pairs):
            exchange(g, k).wait_recv()
            origin = lax.rem(pair - k + pairs, pairs)
            which = jnp.where(origin < pair, 0, 1)
            gap = jnp.where(origin < pair, pair - origin, origin - pair) - 1
            power = jnp.exp(-rate * (gap * (2 * rows)).astype(jnp.float32))
            ca_s[which] += power * held[g, k - 1]
        near = 1 - odd
        ca_s[near] = mate[g, near] + jnp.exp(-rate * rows) * ca_s[near]

    def main(g):
        def chunk(c, _):
            at, inner = places(g, c)
            gates(at)
            rate = jnp.exp(lr_ref[:, at])
            decay = jnp.exp(-rate)
            root = jnp.sqrt(2.0 * rate)
            weight = res_ref[:, at] * root
            carry_in = ca_s[0, :, inner]
            carry_back = ca_s[1, :, inner]
            raw, lag = [], []
            for first in range(0, modes, size):
                group = range(first, first + size)
                a = [wide(decay, m) for m in group]
                w = [wide(weight, m) for m in group]
                s = [
                    sp_s[m, :, at]
                    + jnp.exp(-wide(rate, m) * (span * level)) * wide(carry_in, m)
                    for m in group
                ]
                t = [
                    an_s[m, :, at]
                    + jnp.exp(-wide(rate, m) * (span * (SUB - 1 - level))) * wide(carry_back, m)
                    for m in group
                ]
                rw = [zero] * size
                lg = [zero] * size
                for i in range(span):
                    x = p_s[pl.ds(i, SUB, stride=span), :]
                    y = g_s[pl.ds(i, SUB, stride=span), :]
                    s = [aa * ss + x for aa, ss in zip(a, s)]
                    for j in range(size):
                        s_s[i * size + j] = s[j]
                    rw = [r + y * ss for r, ss in zip(rw, s)]
                    f = total_of([ww * ss for ww, ss in zip(w, s)])
                    if first == 0:
                        f_s[i] = f
                    elif first + size < modes:
                        f_s[i] += f
                    else:
                        fr_s[pl.ds(i, SUB, stride=span), :] = f_s[i] + f
                for i in reversed(range(span)):
                    y = g_s[pl.ds(i, SUB, stride=span), :]
                    lg = [l + s_s[i * size + j] * t[j] for j, l in enumerate(lg)]
                    t = [aa * tt + y for aa, tt in zip(a, t)]
                    b = total_of([ww * tt for ww, tt in zip(w, t)])
                    if first == 0:
                        b_s[i] = b
                    elif first + size < modes:
                        b_s[i] += b
                    else:
                        br_s[pl.ds(i, SUB, stride=span), :] = b_s[i] + b
                raw += [jnp.sum(r, axis=0, keepdims=True) for r in rw]
                lag += [jnp.sum(l, axis=0, keepdims=True) for l in lg]
            for_ref[:, at] = fr_s[...]
            back_ref[:, at] = br_s[...]
            raw_weight = jnp.concatenate(raw, axis=0)
            lag_total = decay * jnp.concatenate(lag, axis=0)
            both = (root * raw_weight, weight * (0.5 * raw_weight - rate * lag_total))
            for piece in range(pieces):
                low = piece % (pieces // 2) * SUB
                raw_s[g, c * pieces + piece] = both[piece // (pieces // 2)][low : low + SUB]
            return 0

        lax.fori_loop(0, per_group, chunk, 0)

    if raw_s.shape[1] > per_group * pieces:
        raw_s[...] = jnp.zeros_like(raw_s)

    def first_stage(g, _):
        ends(g)
        couple(g).start()
        join(g - 1)
        return 0

    def produce(g):
        main(g)
        for k in range(1, n):
            scatter(g, k).start()

    def finish(g):
        mine = raw_s[g, pl.ds(me * own, own)]
        for k in range(1, n):
            scatter(g, k).wait_recv()
            mine = mine + parts[g, k - 1]
        red[g] = mine
        for k in range(1, n):
            gather(g, k).start()
        gath[g, me] = mine
        sums[...] += jnp.sum(mine * mine, axis=0)

    def second_stage(g, _):
        carry(g)
        produce(g)
        finish(g - 1)
        return 0

    sums[...] = zero
    ends(0)
    pl.semaphore_wait(barrier, total - 1)
    couple(0).start()
    lax.fori_loop(1, groups, first_stage, 0)
    if groups == 1:
        join(0)
    carry(0)
    if groups > 1:
        join(groups - 1)
    produce(0)
    lax.fori_loop(1, groups, second_stage, 0)
    finish(groups - 1)
    squares[here] = sums[...]

    def norm_start(q, _):
        norm(q).start()
        return 0

    lax.fori_loop(1, total, norm_start, 0)

    def norm_wait(q, _):
        norm(q).wait()
        return 0

    lax.fori_loop(1, total, norm_wait, 0)
    square = jnp.sum(jnp.sum(squares[...], axis=0), keepdims=True)
    scale = jnp.minimum(1.0, CLIP_NORM / jnp.sqrt(square + 1e-06))
    for g in range(groups):
        for k in range(1, n):
            gather(g, k).wait_recv()
        for c in range(per_group):
            at = pl.ds((g * per_group + c) * LANES, LANES)
            for piece in range(pieces):
                tile = c * pieces + piece
                low = piece % (pieces // 2) * SUB
                ref = dres_ref if piece < pieces // 2 else drate_ref
                ref[low : low + SUB, at] = gath[g, tile // own, tile % own] * scale

    def drain(g, _):
        couple(g).wait_send()
        for k in range(1, pairs):
            exchange(g, k).wait_send()
        for k in range(1, n):
            scatter(g, k).wait_send()
            gather(g, k).wait_send()
        return 0

    lax.fori_loop(0, groups, drain, 0)

def per_device(n, ntp, grad_out, query_in, key_in, value_in, residue, log_rate):
    rows, chans = grad_out.shape
    modes = residue.shape[1]
    span = rows // SUB
    chunks = chans // LANES
    groups = 4 if chunks % 4 == 0 and n <= 32 else 1
    width = chans // groups
    own = -(-(width // LANES * 2 * modes // SUB) // n)
    f32 = jnp.float32
    shape = jax.ShapeDtypeStruct
    vmem = pl.BlockSpec(memory_space=pltpu.VMEM)
    buffer = lambda *dims: pltpu.VMEM(dims, f32)
    tile = lambda *lead: pltpu.VMEM((*lead, SUB, LANES), f32)
    flags = lambda *dims: pltpu.SemaphoreType.DMA(dims)
    flat = buffer(rows, LANES)
    wide_out = shape((rows, chans), f32)
    tall_out = shape((modes, chans), f32)
    filtered, back_filtered, d_res, d_rate = pl.pallas_call(
        functools.partial(fused_kernel, n, ntp, modes, groups),
        out_shape=(wide_out,) * 2 + (tall_out,) * 2,
        in_specs=[vmem] * 6,
        out_specs=(vmem,) * 4,
        scratch_shapes=[
            flat, flat, tile(span), tile(span), tile(8 * span), flat, flat,
            buffer(modes, SUB, chans),
            buffer(modes, SUB, chans),
            buffer(groups, 2, modes, width),
            buffer(groups, 2, modes, width),
            buffer(groups, 2, modes, width),
            buffer(groups, n // 2 - 1, modes, width),
            buffer(2, modes, width),
            tile(groups, own * n),
            tile(groups, n - 1, own),
            tile(groups, own),
            tile(groups, n, own),
            tile(),
            tile(n * ntp),
            flags(groups), flags(groups),
            flags(groups, n // 2 - 1), flags(groups, n // 2 - 1),
            flags(groups, n - 1), flags(groups, n - 1),
            flags(groups, n - 1), flags(groups, n - 1),
            flags(n * ntp - 1), flags(n * ntp - 1),
        ],
        compiler_params=pltpu.CompilerParams(
            collective_id=0, has_side_effects=True, vmem_limit_bytes=VMEM_BYTES
        ),
        name="fused",
    )(grad_out, query_in, key_in, value_in, log_rate.T, residue.T)
    grad_query = (grad_out.astype(f32) * filtered).astype(jnp.bfloat16)
    grad_key = (back_filtered * value_in.astype(f32)).astype(jnp.bfloat16)
    grad_value = (back_filtered * key_in.astype(f32)).astype(jnp.bfloat16)
    return grad_query, grad_key, grad_value, d_res.T, d_rate.T


def solution(mesh):
    wide = P("ctx", "tp")
    tall = P("tp", None)
    body = functools.partial(per_device, mesh.shape["ctx"], mesh.shape["tp"])
    return jax.shard_map(
        body,
        mesh=mesh,
        in_specs=(wide,) * 4 + (tall,) * 2,
        out_specs=(wide,) * 3 + (tall,) * 2,
        check_vma=False,
    )
```
